256 devices in a mesh: lag: 8 (over y, z_lo), row: 32 (over z_hi, x, core).
Axes of the slice: x: 4, y: 4, z: 8 (z_hi: 4, z_lo: 2; z = z_hi * 2 + z_lo), core: 2. Of those that a mesh axis runs over, the one named last changes fastest.
Arguments:
- lag_matrices: bfloat16 [8, 8192, 8192], P('lag', 'row'), may hold values from -0.0234375 to 0.0234375
- history: bfloat16 [8, 8192, 256], P('lag', 'row'), may hold values from -6 to 6
- excitation: float32 [4, 8192, 256], P(None, 'row'), may hold values from -6 to 6
- admittance: float32 [8192], P('row'), may hold values from 0.3 to 1.5
- saturation: float32 [8192], P('row'), may hold values from 0.2 to 1
Outputs:
- densities: bfloat16 [4, 8192, 256], P(None, 'row')
The draws below stay inside these ranges and needn't reach their ends.
All inputs are finite; a program needn't handle non-finite values.
Results may differ from the reference program's by a relative error of at most 0.0023.
Values may be sent and summed in bfloat16 or wider, within the bound.
A program may use at most 128 MiB of HBM per device.

```python
import math
import jax
import jax.numpy as jnp
from jax import lax

UNKNOWNS = 8192
LAGS = 8
COLUMNS = 256
STEPS = 4


def steps_of(key, extent, split, low, top_value):
    def one(dim, blocks):
        draws = jax.random.uniform(jax.random.fold_in(jax.random.fold_in(key, 6), dim), (blocks,), jnp.float32, low / len(split), top_value / len(split))
        return jnp.repeat(jnp.exp(draws), extent[dim] // blocks).reshape((-1,) + (1,) * (len(extent) - dim - 1))

    factor_of = one(*split[0])
    for cut in split[1:]:
        factor_of = factor_of * one(*cut)
    return factor_of


def scatter_about(own_key, dims, width, reach, cuts=(), dtype=jnp.bfloat16):
    values = width * jax.random.normal(own_key, dims, jnp.float32)
    if cuts:
        values = values * steps_of(own_key, dims, cuts, -0.22, 0.18)
    return jnp.clip(values, -reach, reach).astype(dtype)


def setup_inputs(seed: int = 0) -> dict:
    key_list = jax.random.split(jax.random.key(seed), 6)
    return {
        "lag_matrices": scatter_about(key_list[0], (LAGS, UNKNOWNS, UNKNOWNS), (UNKNOWNS * LAGS) ** -0.5, 0.0234375, ((0, 8), (1, 32))),
        "history": scatter_about(key_list[1], (LAGS, UNKNOWNS, COLUMNS), 1.0, 6.0, ((0, 8), (1, 32))),
        "excitation": scatter_about(key_list[2], (STEPS, UNKNOWNS, COLUMNS), 1.0, 6.0, ((1, 32),), jnp.float32),
        "admittance": jnp.clip(jnp.exp(math.log(1.5) - 1.60943787 * jax.random.uniform(key_list[3], (UNKNOWNS,), jnp.float32) ** steps_of(key_list[3], (UNKNOWNS,), ((0, 32),), -0.2, 0.2)), 0.3, 1.5),
        "saturation": jnp.clip(jnp.exp(math.log(1.0) - 1.609438 * jax.random.uniform(key_list[4], (UNKNOWNS,), jnp.float32) ** steps_of(key_list[4], (UNKNOWNS,), ((0, 32),), -0.2, 0.2)), 0.2, 1.0),
    }


def reference(lag_matrices, history, excitation, admittance, saturation):
    history_now = history
    results = []
    admit_col = admittance[:, None]
    satur_col = saturation[:, None]
    for step_index in range(STEPS):

        def add_lag(lag_slot, running):
            return running + jnp.dot(lag_matrices[lag_slot], history_now[lag_slot], preferred_element_type=jnp.float32)
        scattered = lax.fori_loop(0, LAGS, add_lag, jnp.zeros((UNKNOWNS, COLUMNS), jnp.float32))
        drive = excitation[step_index] - scattered
        density = (admit_col * drive / jnp.sqrt(1.0 + (satur_col * drive) ** 2)).astype(jnp.bfloat16)
        results.append(density)
        history_now = jnp.concatenate([density[None], history_now[:-1]], axis=0)
    return jnp.stack(results)
```

```python
import functools

import jax
import jax.numpy as jnp
from jax import lax
from jax.experimental import pallas as pl
from jax.experimental.pallas import tpu as pltpu
from jax.sharding import PartitionSpec as P

MESH = pl.DeviceIdType.MESH
STEPS = 4
LAGS = 8
BLOCK = 256
COLS = 256
PIECE = 32
CHUNK = 1024
NEW = 3


def kernel(
    z_hbm, h_hbm, e_hbm, adm_ref, sat_ref, out_hbm,
    zv, zp, wv, pm, gath, part, rsb, dv, ob, ev,
    s_loc, s_shift, r_shift, s_a, r_z, r_x, r_c, s_w, r_w, s_rs, r_rs, s_d, r_dz, r_dx, r_dc, s_o, r_o, s_out,
):
    lag = lax.axis_index("lag")
    row = lax.axis_index("row")
    zh, x, c = row // 8, (row // 2) % 4, row % 2

    def at(zh_, x_, c_):
        return (lag, zh_ * 8 + x_ * 2 + c_)

    zn = [(zh + k) % 4 for k in range(4)]
    xn = [(x + k) % 4 for k in range(4)]
    up_z, down_z, far_z = at(zn[1], x, c), at(zn[3], x, c), at(zn[2], x, c)
    up_x, down_x, far_x = at(zh, xn[1], c), at(zh, xn[3], c), at(zh, xn[2], c)
    mate = at(zh, x, 1 - c)

    def lag_of(k):
        return (lag + k) % LAGS

    def chunk_of(x_, c_):
        return pl.multiple_of((c_ * 4 + x_) * CHUNK, CHUNK)

    def block_at(zh_, x_, c_):
        return pl.multiple_of(chunk_of(x_, c_) + zh_ * BLOCK, BLOCK)

    def send(src, dst, ss, rs, dev):
        pltpu.make_async_remote_copy(
            src_ref=src, dst_ref=dst, send_sem=ss, recv_sem=rs, device_id=dev, device_id_type=MESH
        ).start()

    def wait(ref, sem):
        pltpu.make_async_copy(ref, ref, sem).wait()

    own = block_at(zh, x, c)
    load_h = pltpu.make_async_copy(h_hbm.at[0], gath.at[0, pl.ds(own, BLOCK)], s_loc.at[0])
    load_h.start()

    def load_z(i, _):
        place = pl.multiple_of(((i % 2) * 16 + ((i // 2) % 4) * 4 + i // 8) * BLOCK, BLOCK)
        pltpu.make_async_copy(
            z_hbm.at[0, :, pl.ds(pl.multiple_of(i * BLOCK, BLOCK), BLOCK)],
            zv.at[:, pl.ds(place, BLOCK)],
            s_loc.at[1],
        ).start()
        return 0

    lax.fori_loop(0, 32, load_z, 0)
    piece = pl.multiple_of(lag * PIECE, PIECE)
    load_e = pltpu.make_async_copy(e_hbm.at[:, pl.ds(piece, PIECE)], ev, s_loc.at[2])
    load_e.start()

    barrier = pltpu.get_barrier_semaphore()
    partners = [up_z, down_z, far_z, up_x, down_x, far_x, mate] + [(lag_of(k), row) for k in range(1, LAGS)]
    for dev in partners:
        pl.semaphore_signal(barrier, inc=1, device_id=dev, device_id_type=MESH)
    part[...] = jnp.zeros_like(part)
    lanes = lax.broadcasted_iota(jnp.int32, (PIECE, BLOCK), 1)
    rows_ = lax.broadcasted_iota(jnp.int32, (PIECE, BLOCK), 0) + lag * PIECE
    mine = lanes == rows_
    admit = jnp.sum(jnp.where(mine, adm_ref[...], 0.0), axis=1, keepdims=True)
    satur = jnp.sum(jnp.where(mine, sat_ref[...], 0.0), axis=1, keepdims=True)
    pl.semaphore_wait(barrier, len(partners))

    tasks = []

    def task(t, fn, cond=None):
        tasks.append((t, fn, cond))

    def g(s, start, size):
        return gath.at[s, pl.ds(start, size)]

    def x_send(s, b, zz):
        src = g(s, block_at(zz, x, c), BLOCK)
        send(src, src, s_a.at[s], r_x.at[s, 0, b], up_x)
        send(src, src, s_a.at[s], r_x.at[s, 1, b], down_x)

    def a_start(s):
        if s == 0:
            load_h.wait()
        else:
            wait(g(s, own, BLOCK), r_shift.at[s])
        src = g(s, own, BLOCK)
        send(src, src, s_a.at[s], r_z.at[s, 0], up_z)
        send(src, src, s_a.at[s], r_z.at[s, 1], down_z)
        x_send(s, 0, zh)

    def shift():
        for s in range(1, STEPS):
            @pl.when(lag + s < LAGS)
            def _():
                send(g(0, own, BLOCK), g(s, own, BLOCK), s_shift.at[s], r_shift.at[s], (lag_of(s), row))

    HALF = BLOCK // 2

    def a_z_low(s):
        wait(g(s, block_at(zn[3], x, c), BLOCK), r_z.at[s, 0])
        src = g(s, block_at(zn[3], x, c), HALF)
        send(src, src, s_a.at[s], r_z.at[s, 2], up_z)
        x_send(s, 1, zn[3])

    def a_z_high(s):
        wait(g(s, block_at(zn[1], x, c), BLOCK), r_z.at[s, 1])
        src = g(s, block_at(zn[1], x, c) + HALF, HALF)
        send(src, src, s_a.at[s], r_z.at[s, 2], down_z)
        x_send(s, 2, zn[1])

    def to_mate(s, j, x_):
        src = g(s, chunk_of(x_, c), CHUNK)
        send(src, src, s_a.at[s], r_c.at[s, j], mate)

    def a_z_far(s):
        wait(g(s, block_at(zn[2], x, c), BLOCK), r_z.at[s, 2])
        x_send(s, 3, zn[2])
        to_mate(s, 0, x)

    order = [0, 3, 1, 2]

    def a_x(s, b):
        zz = zn[order[b]]
        wait(g(s, block_at(zz, xn[3], c), BLOCK), r_x.at[s, 0, b])
        src = g(s, block_at(zz, xn[3], c), HALF)
        send(src, src, s_a.at[s], r_x.at[s, 2, b], up_x)
        wait(g(s, block_at(zz, xn[1], c), BLOCK), r_x.at[s, 1, b])
        src = g(s, block_at(zz, xn[1], c) + HALF, HALF)
        send(src, src, s_a.at[s], r_x.at[s, 2, b], down_x)
        if b == 3:
            to_mate(s, 1, xn[3])
            to_mate(s, 2, xn[1])

    def a_x_far(s):
        for b in range(4):
            wait(g(s, block_at(zn[order[b]], xn[2], c), BLOCK), r_x.at[s, 2, b])
        to_mate(s, 3, xn[2])

    def multiply(s, js):
        for j in js:
            wait(g(s, chunk_of(xn[order[j]], 1 - c), CHUNK), r_c.at[s, j])

        def body(t, _):
            step = 2 if js == [3] else 3 * (t // 2) + 3 * (t // 4)
            at_ = chunk_of((x + step) % 4, t % 2)
            part[s] += jnp.dot(
                zv[:, pl.ds(at_, CHUNK)], gath[s, pl.ds(at_, CHUNK), :], preferred_element_type=jnp.float32
            )
            return 0

        lax.fori_loop(0, 2 * len(js), body, 0)

    def a_first(s):
        multiply(s, [0, 1, 2])

    def a_last(s):
        multiply(s, [3])

    def w_send():
        a = lax.broadcasted_iota(jnp.int32, (CHUNK, CHUNK), 0)
        b = lax.broadcasted_iota(jnp.int32, (CHUNK, CHUNK), 1)
        from_ = ((b // PIECE) % 4) * BLOCK + (b // 128) * PIECE + b % PIECE
        pm[...] = jnp.where(a == from_, 1.0, 0.0).astype(jnp.bfloat16)

        def body(q, _):
            picked = jnp.dot(
                zv[:, pl.ds(pl.multiple_of(q * CHUNK, CHUNK), CHUNK)], pm[...], preferred_element_type=jnp.float32
            ).astype(jnp.bfloat16)
            for k in range(LAGS):
                zp[k, :, pl.ds(pl.multiple_of(q * 128, 128), 128)] = picked[:, k * 128 : (k + 1) * 128]
            return 0

        lax.fori_loop(0, LAGS, body, 0)
        pltpu.make_async_copy(zp.at[lag], wv.at[lag], r_w.at[lag]).start()
        for k in range(1, LAGS):
            send(zp.at[lag_of(k)], wv.at[lag], s_w.at[0], r_w.at[lag], (lag_of(k), row))

    def rs_send(n):
        for k in range(1, LAGS):
            to = lag_of(k)
            send(
                part.at[n, pl.ds(pl.multiple_of(to * PIECE, PIECE), PIECE)],
                rsb.at[n, lag], s_rs.at[n], r_rs.at[n], (to, row),
            )
        rsb[n, lag] = part[n, pl.ds(piece, PIECE), :]

    def d_at(zh_, x_):
        return pl.multiple_of((c * 4 + x_) * 128 + zh_ * PIECE, PIECE)

    def new_density(n):
        wait(rsb.at[n, pl.ds(0, LAGS - 1)], r_rs.at[n])
        total = rsb[n, 0]
        for k in range(1, LAGS):
            total = total + rsb[n, k]
        drive = ev[n] - total
        density = (admit * drive / jnp.sqrt(1.0 + (satur * drive) ** 2)).astype(jnp.bfloat16)
        ob[n, pl.ds(piece, PIECE), :] = density
        if n < STEPS - 1:
            dv[n, pl.ds(d_at(zh, x), PIECE), :] = density
            src = dv.at[n, pl.ds(d_at(zh, x), PIECE)]
            send(src, src, s_d.at[n], r_dz.at[n], far_z)
            send(src, src, s_d.at[n], r_dz.at[n], up_z)
            send(src, src, s_d.at[n], r_dz.at[n], down_z)
        src = ob.at[n, pl.ds(piece, PIECE)]
        for k in range(1, LAGS):
            send(src, src, s_o.at[n], r_o.at[n], (lag_of(k), row))

    def d_chunk(n, x_, c_):
        return dv.at[n, pl.ds(pl.multiple_of((c_ * 4 + x_) * 128, 128), 128)]

    def d_x(n):
        wait(dv.at[n, pl.ds(0, 3 * PIECE)], r_dz.at[n])
        src = d_chunk(n, x, c)
        send(src, src, s_d.at[n], r_dx.at[n], far_x)
        send(src, src, s_d.at[n], r_dx.at[n], up_x)
        send(src, src, s_d.at[n], r_dx.at[n], down_x)

    def d_c(n):
        wait(dv.at[n, pl.ds(0, 3 * 128)], r_dx.at[n])
        src = dv.at[n, pl.ds(pl.multiple_of(c * 512, 512), 512)]
        send(src, src, s_d.at[n], r_dc.at[n], mate)

    def w_mul(n, k):
        part[n + 1 + k] += jnp.dot(wv[k], dv[n], preferred_element_type=jnp.float32)

    def d_first(n):
        wait(dv.at[n, pl.ds(0, 512)], r_dc.at[n])
        if n == 0:
            wait(wv.at[0], r_w.at[0])
        w_mul(n, 0)

    def d_rest(n):
        if n == 0:
            wait(wv.at[1], r_w.at[1])
            wait(wv.at[2], r_w.at[2])
        for k in range(1, STEPS - 1 - n):
            w_mul(n, k)

    task(0, functools.partial(a_start, 0))
    task(0.5, shift)

    def z_ready():
        wait(zv, s_loc.at[1])
        load_e.wait()

    task(1, z_ready)
    task(2, w_send, lag < NEW)
    begin = [0, 8, 22, 36]
    for s in range(STEPS):
        cond = None if s == 0 else (lag >= s)
        t = begin[s]
        if s:
            task(t, functools.partial(a_start, s), cond)
        task(t + 5, functools.partial(a_z_low, s), cond)
        task(t + 5.1, functools.partial(a_z_high, s), cond)
        task(t + 8, functools.partial(a_z_far, s), cond)
        for b in range(4):
            task(t + [6, 10, 12, 16][b], functools.partial(a_x, s, b), cond)
        task(t + 17, functools.partial(a_first, s), cond)
        task(t + 19, functools.partial(a_x_far, s), cond)
        task(t + 20, functools.partial(a_last, s), cond)
    ready = 20.5
    for n in range(STEPS):
        task(ready, functools.partial(rs_send, n))
        task(ready + 4, functools.partial(new_density, n))
        if n < STEPS - 1:
            task(ready + 8, functools.partial(d_x, n))
            task(ready + 11, functools.partial(d_c, n))
            task(ready + 12.5, functools.partial(d_first, n))
            task(ready + 13.5, functools.partial(d_rest, n))
            ready = max(ready + 13, begin[n + 1] + 20.4)
    for t, fn, cond in sorted(tasks, key=lambda item: item[0]):
        if cond is None:
            fn()
        else:
            pl.when(cond)(fn)

    for n in range(STEPS):
        wait(ob.at[n, pl.ds(0, (LAGS - 1) * PIECE)], r_o.at[n])
    store = pltpu.make_async_copy(ob, out_hbm, s_out.at[0])
    store.start()
    for n in range(STEPS):
        wait(rsb.at[n, pl.ds(0, LAGS - 1)], s_rs.at[n])
        wait(ob.at[n, pl.ds(0, (LAGS - 1) * PIECE)], s_o.at[n])
        if n < STEPS - 1:
            wait(dv.at[n, pl.ds(0, 3 * PIECE + 3 * 128 + 512)], s_d.at[n])
    for s in range(STEPS):
        def done(s=s):
            wait(g(s, 0, 3 * BLOCK + 12 * BLOCK + 4 * CHUNK), s_a.at[s])

        if s == 0:
            done()
        else:
            pl.when(lag >= s)(done)

            @pl.when(lag + s < LAGS)
            def _():
                wait(g(0, 0, BLOCK), s_shift.at[s])

    @pl.when(lag < NEW)
    def _():
        wait(zp.at[pl.ds(0, LAGS - 1)], s_w.at[0])

    store.wait()


def body(lag_matrices, history, excitation, admittance, saturation):
    dma = pltpu.SemaphoreType.DMA
    any_ = pl.BlockSpec(memory_space=pl.ANY)
    vmem = pl.BlockSpec(memory_space=pltpu.VMEM)
    return pl.pallas_call(
        kernel,
        out_shape=jax.ShapeDtypeStruct((STEPS, BLOCK, COLS), jnp.bfloat16),
        in_specs=[any_, any_, any_, vmem, vmem],
        out_specs=any_,
        scratch_shapes=[
            pltpu.VMEM((BLOCK, 8192), jnp.bfloat16),
            pltpu.VMEM((LAGS, BLOCK, CHUNK), jnp.bfloat16),
            pltpu.VMEM((NEW, BLOCK, CHUNK), jnp.bfloat16),
            pltpu.VMEM((CHUNK, CHUNK), jnp.bfloat16),
            pltpu.VMEM((STEPS, 8192, COLS), jnp.bfloat16),
            pltpu.VMEM((STEPS, BLOCK, COLS), jnp.float32),
            pltpu.VMEM((STEPS, LAGS, PIECE, COLS), jnp.float32),
            pltpu.VMEM((STEPS - 1, CHUNK, COLS), jnp.bfloat16),
            pltpu.VMEM((STEPS, BLOCK, COLS), jnp.bfloat16),
            pltpu.VMEM((STEPS, PIECE, COLS), jnp.float32),
            dma((3,)),
            dma((STEPS,)), dma((STEPS,)),
            dma((STEPS,)), dma((STEPS, 3)), dma((STEPS, 3, 4)), dma((STEPS, 4)),
            dma((1,)), dma((NEW,)),
            dma((STEPS,)), dma((STEPS,)),
            dma((STEPS,)), dma((STEPS,)), dma((STEPS,)), dma((STEPS,)),
            dma((STEPS,)), dma((STEPS,)),
            dma((1,)),
        ],
        compiler_params=pltpu.CompilerParams(
            collective_id=0, has_side_effects=True, vmem_limit_bytes=60 * 1024 * 1024
        ),
    )(
        lag_matrices, history, excitation, admittance.reshape(1, BLOCK), saturation.reshape(1, BLOCK)
    )


def solution(mesh):
    placed = (
        P("lag", "row", None),
        P("lag", "row", None),
        P(None, "row", None),
        P("row"),
        P("row"),
    )
    return jax.shard_map(
        body, mesh=mesh, in_specs=placed, out_specs=P(None, "row", None), check_vma=False
    )
```

```python
import functools

import jax
import jax.numpy as jnp
from jax import lax
from jax.experimental import pallas as pl
from jax.experimental.pallas import tpu as pltpu
from jax.sharding import PartitionSpec as P

MESH = pl.DeviceIdType.MESH
STEPS = 4
LAGS = 8
BLOCK = 256
COLS = 256
ZT = (0, 7, 7.1, 11)
Z_AT = (0, 13, 39.2, 57.2)
X_AT = ((0, 8, 12, 17), (23, 27, 31, 35), (46, 50, 54, 58), (62, 66, 70, 74))
X_LAG = 5
Y_AT = (26, 3, 6)
C_AT = (26, 45, 62, 79)
W_RELAY = 20
PIECE = 32
CHUNK = 1024


def kernel(
    z_hbm, h_hbm, e_hbm, adm_ref, sat_ref, out_hbm,
    zv, zp, wv, gath, part, rsb, dv, ob, ev,
    s_loc, s_shift, r_shift, s_a, r_z, r_x, r_c, s_y, r_y, s_w, r_w, s_rs, r_rs, s_d, r_dz, r_dx, r_dc, s_o, r_o, s_out,
):
    lag = lax.axis_index("lag")
    row = lax.axis_index("row")
    zh, x, c = row // 8, (row // 2) % 4, row % 2

    def at(zh_, x_, c_):
        return (lag, zh_ * 8 + x_ * 2 + c_)

    zn = [(zh + k) % 4 for k in range(4)]
    xn = [(x + k) % 4 for k in range(4)]
    up_z, down_z, far_z = at(zn[1], x, c), at(zn[3], x, c), at(zn[2], x, c)
    up_x, down_x, far_x = at(zh, xn[1], c), at(zh, xn[3], c), at(zh, xn[2], c)
    mate = at(zh, x, 1 - c)

    def lag_of(k):
        return (lag + k) % LAGS

    def chunk_of(x_, c_):
        return pl.multiple_of((c_ * 4 + x_) * CHUNK, CHUNK)

    def block_at(zh_, x_, c_):
        return pl.multiple_of(chunk_of(x_, c_) + zh_ * BLOCK, BLOCK)

    def send(src, dst, ss, rs, dev):
        pltpu.make_async_remote_copy(
            src_ref=src, dst_ref=dst, send_sem=ss, recv_sem=rs, device_id=dev, device_id_type=MESH
        ).start()

    def wait(ref, sem):
        pltpu.make_async_copy(ref, ref, sem).wait()

    own = block_at(zh, x, c)
    load_h = pltpu.make_async_copy(h_hbm.at[0], gath.at[0, pl.ds(own, BLOCK)], s_loc.at[0])
    load_h.start()

    def load_z(i, _):
        place = pl.multiple_of(((i % 2) * 16 + ((i // 2) % 4) * 4 + i // 8) * BLOCK, BLOCK)
        pltpu.make_async_copy(
            z_hbm.at[0, :, pl.ds(pl.multiple_of(i * BLOCK, BLOCK), BLOCK)],
            zv.at[:, pl.ds(place, BLOCK)],
            s_loc.at[1],
        ).start()
        return 0

    lax.fori_loop(0, 32, load_z, 0)
    piece = pl.multiple_of(lag * PIECE, PIECE)
    load_e = pltpu.make_async_copy(e_hbm.at[:, pl.ds(piece, PIECE)], ev, s_loc.at[2])
    load_e.start()

    barrier = pltpu.get_barrier_semaphore()
    partners = [up_z, down_z, far_z, up_x, down_x, far_x, mate] + [(lag_of(k), row) for k in range(1, LAGS)]
    for dev in partners:
        pl.semaphore_signal(barrier, inc=1, device_id=dev, device_id_type=MESH)
    part[...] = jnp.zeros_like(part)
    lanes = lax.broadcasted_iota(jnp.int32, (PIECE, BLOCK), 1)
    rows_ = lax.broadcasted_iota(jnp.int32, (PIECE, BLOCK), 0) + lag * PIECE
    mine = lanes == rows_
    admit = jnp.sum(jnp.where(mine, adm_ref[...], 0.0), axis=1, keepdims=True)
    satur = jnp.sum(jnp.where(mine, sat_ref[...], 0.0), axis=1, keepdims=True)
    pl.semaphore_wait(barrier, len(partners))

    order = [0, 3, 1, 2]
    tasks = []

    def task(t, fn, cond=None):
        tasks.append((t, fn, cond))

    def g(s, start, size):
        return gath.at[s, pl.ds(start, size)]

    def x_send(s, b):
        src = g(s, block_at(zn[order[b]], x, c), BLOCK)
        send(src, src, s_a.at[s], r_x.at[s, 0, b], up_x)
        send(src, src, s_a.at[s], r_x.at[s, 1, b], down_x)

    def a_start(s):
        if s == 0:
            load_h.wait()
        elif s < 3:
            @pl.when(lag >= s)
            def _():
                wait(g(s, own, BLOCK), r_shift.at[s])
        if s >= 2:
            @pl.when(lag == s - 1)
            def _():
                gath[s, pl.ds(own, BLOCK), :] = ob[0]
        if s == 3:
            @pl.when(lag == 1)
            def _():
                gath[s, pl.ds(own, BLOCK), :] = ob[1]

        src = g(s, own, BLOCK)
        send(src, src, s_a.at[s], r_z.at[s, 0], up_z)
        send(src, src, s_a.at[s], r_z.at[s, 1], down_z)
        send(src, src, s_a.at[s], r_z.at[s, 2], far_z)

    def shift():
        for s in (1, 2):
            @pl.when(lag + s < LAGS)
            def _():
                send(g(0, own, BLOCK), g(s, own, BLOCK), s_shift.at[s], r_shift.at[s], (lag_of(s), row))

    HALF = BLOCK // 2

    def to_mate(s, j, x_):
        src = g(s, chunk_of(x_, c), CHUNK)
        send(src, src, s_a.at[s], r_c.at[s, j], mate)

    def to_y(j, b):
        start = block_at(zn[order[b]], xn[order[j]], c)
        send(g(1, start, BLOCK), g(3, start, BLOCK), s_y.at[0], r_y.at[(0, 1, 1, 2)[j]], (lag_of(2), row))

    def from_y(i):
        wait(g(3, 0, (1, 2, 1)[i] * CHUNK), r_y.at[i])
        for j in ((0,), (1, 2), (3,))[i]:
            to_mate(3, j, xn[order[j]])

    def a_z(s, b):
        wait(g(s, block_at(zn[order[b]], x, c), BLOCK), r_z.at[s, b - 1])
        if b == 3:
            to_mate(s, 0, x)

    def a_x(s, b):
        zz = zn[order[b]]
        wait(g(s, block_at(zz, xn[3], c), BLOCK), r_x.at[s, 0, b])
        src = g(s, block_at(zz, xn[3], c), HALF)
        send(src, src, s_a.at[s], r_x.at[s, 2, b], up_x)
        wait(g(s, block_at(zz, xn[1], c), BLOCK), r_x.at[s, 1, b])
        src = g(s, block_at(zz, xn[1], c) + HALF, HALF)
        send(src, src, s_a.at[s], r_x.at[s, 2, b], down_x)
        if b == 3:
            to_mate(s, 1, xn[3])
            to_mate(s, 2, xn[1])

    def a_x_far(s):
        for b in range(4):
            wait(g(s, block_at(zn[order[b]], xn[2], c), BLOCK), r_x.at[s, 2, b])
        to_mate(s, 3, xn[2])

    def multiply(s, j):
        wait(g(s, chunk_of(xn[order[j]], 1 - c), CHUNK), r_c.at[s, j])

        def body(t, _):
            at_ = chunk_of(xn[order[j]], t)
            part[s] += jnp.dot(
                zv[:, pl.ds(at_, CHUNK)], gath[s, pl.ds(at_, CHUNK), :], preferred_element_type=jnp.float32
            )
            return 0

        lax.fori_loop(0, 2, body, 0)

    def w_cut():
        place = lax.broadcasted_iota(jnp.int32, (BLOCK, 128), 1) // PIECE

        def body(q, _):
            for half in range(2):
                tiles = []
                for b in range(4):
                    at_ = pl.multiple_of(q * CHUNK + b * BLOCK + half * 128, 128)
                    tile = zv[:, pl.ds(at_, 128)].astype(jnp.float32)
                    tiles.append(pltpu.roll(tile, PIECE * b, 1) if b else tile)
                for a in range(4):
                    got = tiles[(0 - a) % 4]
                    for p in range(1, 4):
                        got = jnp.where(place == p, tiles[(p - a) % 4], got)
                    zp[4 * half + a, :, pl.ds(pl.multiple_of(q * 128, 128), 128)] = got.astype(jnp.bfloat16)
            return 0

        lax.fori_loop(0, LAGS, body, 0)

    def w_send():
        pltpu.make_async_copy(zp.at[0], wv, r_w.at[0]).start()
        for k in (3, 7):
            send(zp.at[k], zp.at[0], s_w.at[0], r_w.at[1], (k - 1, row))
        for k in (4, 5, 2, 6, 1):
            send(zp.at[k], wv, s_w.at[0], r_w.at[0], (k, row))

    def w_relay():
        wait(zp.at[0], r_w.at[1])
        send(zp.at[0], wv, s_w.at[0], r_w.at[0], (lag_of(1), row))

    def rs_send(n):
        for k in range(1, LAGS):
            to = lag_of(k)
            send(
                part.at[n, pl.ds(pl.multiple_of(to * PIECE, PIECE), PIECE)],
                rsb.at[n, lag], s_rs.at[n], r_rs.at[n], (to, row),
            )
        rsb[n, lag] = part[n, pl.ds(piece, PIECE), :]

    def d_at(zh_, x_):
        return pl.multiple_of((c * 4 + x_) * 128 + ((zh_ + lag) % 4) * PIECE, PIECE)

    def new_density(n):
        wait(rsb.at[n, pl.ds(0, LAGS - 1)], r_rs.at[n])
        total = rsb[n, 0]
        for k in range(1, LAGS):
            total = total + rsb[n, k]
        drive = ev[n] - total
        density = (admit * drive / jnp.sqrt(1.0 + (satur * drive) ** 2)).astype(jnp.bfloat16)
        ob[n, pl.ds(piece, PIECE), :] = density
        if n < STEPS - 1:
            dv[n, pl.ds(d_at(zh, x), PIECE), :] = density
            src = dv.at[n, pl.ds(d_at(zh, x), PIECE)]
            send(src, src, s_d.at[n], r_dz.at[n, 0], far_z)
            send(src, src, s_d.at[n], r_dz.at[n, 1], up_z)
            send(src, src, s_d.at[n], r_dz.at[n, 2], down_z)
            d_send_x(n, 0)
        src = ob.at[n, pl.ds(piece, PIECE)]
        for k in range(1, LAGS):
            send(src, src, s_o.at[n], r_o.at[n], (lag_of(k), row))

    def d_send_x(n, b):
        src = d_piece(n, b)
        for dev in (far_x, up_x, down_x):
            send(src, src, s_d.at[n], r_dx.at[n, b], dev)

    def d_piece(n, b):
        return dv.at[n, pl.ds(d_at(zn[order[b]], x), PIECE)]

    def d_near(n):
        wait(d_piece(n, 1), r_dz.at[n, 1])
        d_send_x(n, 1)
        wait(d_piece(n, 2), r_dz.at[n, 2])
        d_send_x(n, 2)

    def d_far(n):
        wait(d_piece(n, 3), r_dz.at[n, 0])
        d_send_x(n, 3)

    def d_c(n):
        for b in range(4):
            wait(dv.at[n, pl.ds(0, 3 * PIECE)], r_dx.at[n, b])
        src = dv.at[n, pl.ds(pl.multiple_of(c * 512, 512), 512)]
        send(src, src, s_d.at[n], r_dc.at[n], mate)

    def d_mul(n):
        wait(dv.at[n, pl.ds(0, 512)], r_dc.at[n])
        if n == 0:
            wait(wv, r_w.at[0])
        part[n + 1] += jnp.dot(wv[...], dv[n], preferred_element_type=jnp.float32)

    def o_ready(n):
        wait(ob.at[n, pl.ds(0, (LAGS - 1) * PIECE)], r_o.at[n])

    def z_ready():
        wait(zv, s_loc.at[1])
        load_e.wait()

    ends = [0] * STEPS

    def gather(s, tz, x_at, x_lag, cond=None):
        def add(t, fn, *more):
            task(t, functools.partial(fn, s, *more), cond)

        add(tz, a_start)
        for b in range(1, 4):
            add(tz + ZT[b], a_z, b)
        add(tz + ZT[3] + 2, multiply, 0)
        for b in range(4):
            add(max(x_at[b], tz + ZT[b]) + 0.001, x_send, b)
            add(x_at[b] + x_lag, a_x, b)
        last = x_at[3] + x_lag
        add(last + 1.5, multiply, 1)
        add(last + 1.6, multiply, 2)
        add(last + 2, a_x_far)
        add(last + 3.5, multiply, 3)
        ends[s] = max(ends[s], last + 3.6)

    gather(0, 0, X_AT[0], 5)
    task(0.5, shift)
    task(1, z_ready)
    task(1.1, w_cut, lag == 0)
    task(1.2, w_send, lag == 0)
    task(W_RELAY, w_relay, (lag == 2) | (lag == 6))
    gather(1, Z_AT[1], X_AT[1], X_LAG, lag >= 1)
    gather(2, Z_AT[2], X_AT[2], X_LAG, lag >= 1)
    gather(3, Z_AT[3], X_AT[3], X_LAG, (lag == 1) | (lag == 2))
    blocks = [(0, b) for b in range(4)] + [(j, b) for b in range(4) for j in (1, 2)] + [(3, b) for b in range(4)]
    for i, (j, b) in enumerate(blocks):
        task(Y_AT[0] + Y_AT[1] * i, functools.partial(to_y, j, b), (lag >= 1) & (lag + 2 < LAGS))
    for i in range(3):
        t = Y_AT[0] + Y_AT[1] * (3, 11, 15)[i] + Y_AT[2]
        task(t, functools.partial(from_y, i), lag >= 3)
        for j in ((0,), (1, 2), (3,))[i]:
            task(t + 2, functools.partial(multiply, 3, j), lag >= 3)
        ends[3] = max(ends[3], t + 2.1)
    for n in range(STEPS):
        ready = max(C_AT[n], ends[n])
        task(ready, functools.partial(rs_send, n))
        task(ready + 6, functools.partial(new_density, n))
        task(ready + 11, functools.partial(o_ready, n))
        if n < STEPS - 1:
            task(ready + 9, functools.partial(d_near, n))
            task(ready + 10.5, functools.partial(d_far, n))
            task(ready + 14, functools.partial(d_c, n))
            task(ready + 15.5, functools.partial(d_mul, n))
            ends[n + 1] = max(ends[n + 1], ready + 15.6)
            if n < 2:
                assert Z_AT[n + 2] > ready + 11
    for t, fn, cond in sorted(tasks, key=lambda item: item[0]):
        if cond is None:
            fn()
        else:
            pl.when(cond)(fn)

    store = pltpu.make_async_copy(ob, out_hbm, s_out.at[0])
    store.start()
    for n in range(STEPS):
        wait(rsb.at[n, pl.ds(0, LAGS - 1)], s_rs.at[n])
        wait(ob.at[n, pl.ds(0, (LAGS - 1) * PIECE)], s_o.at[n])
        if n < STEPS - 1:
            wait(dv.at[n, pl.ds(0, 3 * PIECE + 12 * PIECE + 512)], s_d.at[n])
    for s in range(STEPS):
        def done(s=s):
            wait(g(s, 0, 3 * BLOCK + 12 * BLOCK + 4 * CHUNK), s_a.at[s])

        if s == 0:
            done()
        else:
            pl.when((lag >= 1) & (lag < 3) if s == 3 else lag >= 1)(done)
            if s == 3:
                @pl.when(lag >= 3)
                def _():
                    wait(g(s, 0, 4 * CHUNK), s_a.at[s])
                continue

            @pl.when(lag + s < LAGS)
            def _():
                wait(g(0, 0, BLOCK), s_shift.at[s])

    @pl.when((lag >= 1) & (lag + 2 < LAGS))
    def _():
        wait(g(3, 0, 4 * CHUNK), s_y.at[0])

    @pl.when((lag == 2) | (lag == 6))
    def _():
        wait(zp.at[0], s_w.at[0])

    @pl.when(lag == 0)
    def _():
        wait(zp.at[pl.ds(0, LAGS - 1)], s_w.at[0])

    store.wait()


def body(lag_matrices, history, excitation, admittance, saturation):
    dma = pltpu.SemaphoreType.DMA
    any_ = pl.BlockSpec(memory_space=pl.ANY)
    vmem = pl.BlockSpec(memory_space=pltpu.VMEM)
    return pl.pallas_call(
        kernel,
        out_shape=jax.ShapeDtypeStruct((STEPS, BLOCK, COLS), jnp.bfloat16),
        in_specs=[any_, any_, any_, vmem, vmem],
        out_specs=any_,
        scratch_shapes=[
            pltpu.VMEM((BLOCK, 8192), jnp.bfloat16),
            pltpu.VMEM((LAGS, BLOCK, CHUNK), jnp.bfloat16),
            pltpu.VMEM((BLOCK, CHUNK), jnp.bfloat16),
            pltpu.VMEM((STEPS, 8192, COLS), jnp.bfloat16),
            pltpu.VMEM((STEPS, BLOCK, COLS), jnp.float32),
            pltpu.VMEM((STEPS, LAGS, PIECE, COLS), jnp.float32),
            pltpu.VMEM((STEPS - 1, CHUNK, COLS), jnp.bfloat16),
            pltpu.VMEM((STEPS, BLOCK, COLS), jnp.bfloat16),
            pltpu.VMEM((STEPS, PIECE, COLS), jnp.float32),
            dma((3,)),
            dma((STEPS,)), dma((STEPS,)),
            dma((STEPS,)), dma((STEPS, 3)), dma((STEPS, 3, 4)), dma((STEPS, 4)),
            dma((1,)), dma((3,)),
            dma((1,)), dma((2,)),
            dma((STEPS,)), dma((STEPS,)),
            dma((STEPS,)), dma((STEPS, 3)), dma((STEPS, 4)), dma((STEPS,)),
            dma((STEPS,)), dma((STEPS,)),
            dma((1,)),
        ],
        compiler_params=pltpu.CompilerParams(
            collective_id=0, has_side_effects=True, vmem_limit_bytes=60 * 1024 * 1024
        ),
    )(
        lag_matrices, history, excitation, admittance.reshape(1, BLOCK), saturation.reshape(1, BLOCK)
    )


def solution(mesh):
    placed = (
        P("lag", "row", None),
        P("lag", "row", None),
        P(None, "row", None),
        P("row"),
        P("row"),
    )
    return jax.shard_map(
        body, mesh=mesh, in_specs=placed, out_specs=P(None, "row", None), check_vma=False
    )
```

```python
import functools

import jax
import jax.numpy as jnp
from jax import lax
from jax.experimental import pallas as pl
from jax.experimental.pallas import tpu as pltpu
from jax.sharding import PartitionSpec as P

MESH = pl.DeviceIdType.MESH
STEPS = 4
LAGS = 8
BLOCK = 256
COLS = 256
ROUTED = (0,)
FAR_FIRST = (4, 5, 3, 2, 6, 1, 7)
ORDER = (
    ("own", 0), ("start", 0), ("x", 0, 0), "shift", "z", "cut", "cut_out", ("along_z", 0, 1), ("along_z", 0, 2),
    ("x", 0, 1), ("own", 1), ("start", 1), ("along_z", 0, 3), ("x", 0, 2), ("mul", 0, 0), ("x", 0, 3),
    ("along_z", 1, 1), ("along_z", 1, 2), ("x", 1, 0), ("y", 0, 0), "relay", ("along_z", 1, 3), ("y", 0, 1),
    ("x", 1, 1), ("along_x", 0, 0), ("along_x", 0, 1), ("along_x", 0, 2), ("along_x", 0, 3), ("mul", 0, 1),
    ("mul", 0, 2), ("far_x", 0), ("mul", 0, 3), ("sum", 0), ("y", 0, 2), ("mul", 1, 0), ("x", 1, 2), ("along_x", 1, 0),
    ("y", 0, 3), ("x", 1, 3), ("along_x", 1, 1), ("density", 0), ("out", 0), ("y", 1, 0), ("near", 0),
    ("along_x", 1, 2), ("y", 2, 0), ("far", 0), ("outs", 0), ("own", 2), ("start", 2), ("own", 3), ("start", 3),
    ("y", 1, 1), ("along_x", 1, 3), ("mate", 0), ("along_y", 0), ("mul", 1, 1), ("new", 0), ("mul", 1, 2), ("far_x", 1),
    ("mul", "y", 0), ("y", 2, 1), ("mul", 1, 3), ("sum", 1), ("x", 2, 0), ("x", 3, 0), ("along_z", 2, 1),
    ("along_z", 3, 1), ("along_z", 2, 2), ("along_z", 3, 2), ("y", 1, 2), ("x", 2, 1), ("x", 3, 1), ("y", 2, 2),
    ("along_z", 2, 3), ("along_z", 3, 3), ("along_x", 2, 0), ("density", 1), ("along_x", 3, 0), ("out", 1),
    ("mul", 2, 0), ("mul", 3, 0), ("near", 1), ("y", 1, 3), ("x", 2, 2), ("x", 3, 2), ("along_x", 2, 1),
    ("along_x", 3, 1), ("far", 1), ("outs", 1), ("y", 2, 3), ("own", 4), ("start", 4), ("x", 2, 3), ("x", 3, 3),
    ("along_x", 2, 2), ("mate", 1), ("along_x", 3, 2), ("y", 3, 0), ("new", 1), ("x", 4, 0), ("along_x", 2, 3),
    ("along_x", 3, 3), ("y", 3, 1), ("along_z", 4, 1), ("along_z", 4, 2), ("mul", 2, 1), ("mul", 3, 1), ("mul", 2, 2),
    ("mul", 3, 2), ("along_y", 1), ("far_x", 2), ("far_x", 3), ("x", 4, 1), ("mul", 2, 3), ("mul", 3, 3), ("sum", 2),
    ("along_x", 4, 0), ("mul", "y", 1), ("mul", "y", 2), ("y", 3, 2), ("along_z", 4, 3), ("x", 4, 2), ("mul", 4, 0),
    ("y", 3, 3), ("along_x", 4, 1), ("density", 2), ("out", 2), ("x", 4, 3), ("along_x", 4, 2), ("near", 2),
    ("along_y", 2), ("far", 2), ("outs", 2), ("along_x", 4, 3), ("mul", "y", 3), ("mul", 4, 1), ("mate", 2),
    ("mul", 4, 2), ("far_x", 4), ("new", 2), ("mul", 4, 3), ("sum", 3), ("density", 3), ("out", 3), ("outs", 3),
)
PIECE = 32
CHUNK = 1024


def kernel(
    z_hbm, h_hbm, e_hbm, adm_ref, sat_ref, out_hbm,
    zv, zp, wv, gath, part, rsb, dv, ob, ev,
    s_loc, s_shift, r_shift, s_a, r_z, r_x, r_c, s_y, r_y, s_w, r_w, s_rs, r_rs, s_d, r_dz, r_dx, r_dc, s_o, r_o, s_out,
):
    lag = lax.axis_index("lag")
    row = lax.axis_index("row")
    zh, x, c = row // 8, (row // 2) % 4, row % 2

    def at(zh_, x_, c_):
        return (lag, zh_ * 8 + x_ * 2 + c_)

    zn = [(zh + k) % 4 for k in range(4)]
    xn = [(x + k) % 4 for k in range(4)]
    up_z, down_z, far_z = at(zn[1], x, c), at(zn[3], x, c), at(zn[2], x, c)
    up_x, down_x, far_x = at(zh, xn[1], c), at(zh, xn[3], c), at(zh, xn[2], c)
    mate = at(zh, x, 1 - c)

    def lag_of(k):
        return (lag + k) % LAGS

    def chunk_of(x_, c_):
        return pl.multiple_of((c_ * 4 + x_) * CHUNK, CHUNK)

    def block_at(zh_, x_, c_):
        return pl.multiple_of(chunk_of(x_, c_) + zh_ * BLOCK, BLOCK)

    def send(src, dst, ss, rs, dev):
        pltpu.make_async_remote_copy(
            src_ref=src, dst_ref=dst, send_sem=ss, recv_sem=rs, device_id=dev, device_id_type=MESH
        ).start()

    def wait(ref, sem):
        pltpu.make_async_copy(ref, ref, sem).wait()

    own = block_at(zh, x, c)
    load_h = pltpu.make_async_copy(h_hbm.at[0], gath.at[0, pl.ds(own, BLOCK)], s_loc.at[0])
    load_h.start()

    def load_z(i, _):
        place = pl.multiple_of(((i % 2) * 16 + ((i // 2) % 4) * 4 + i // 8) * BLOCK, BLOCK)
        pltpu.make_async_copy(
            z_hbm.at[0, :, pl.ds(pl.multiple_of(i * BLOCK, BLOCK), BLOCK)],
            zv.at[:, pl.ds(place, BLOCK)],
            s_loc.at[1],
        ).start()
        return 0

    lax.fori_loop(0, 32, load_z, 0)
    piece = pl.multiple_of(lag * PIECE, PIECE)
    load_e = pltpu.make_async_copy(e_hbm.at[:, pl.ds(piece, PIECE)], ev, s_loc.at[2])
    load_e.start()

    barrier = pltpu.get_barrier_semaphore()
    partners = [up_z, down_z, far_z, up_x, down_x, far_x, mate] + [(lag_of(k), row) for k in range(1, LAGS)]
    for dev in partners:
        pl.semaphore_signal(barrier, inc=1, device_id=dev, device_id_type=MESH)
    part[...] = jnp.zeros_like(part)
    lanes = lax.broadcasted_iota(jnp.int32, (PIECE, BLOCK), 1)
    rows_ = lax.broadcasted_iota(jnp.int32, (PIECE, BLOCK), 0) + lag * PIECE
    mine = lanes == rows_
    admit = jnp.sum(jnp.where(mine, adm_ref[...], 0.0), axis=1, keepdims=True)
    satur = jnp.sum(jnp.where(mine, sat_ref[...], 0.0), axis=1, keepdims=True)
    pl.semaphore_wait(barrier, len(partners))

    order = [0, 3, 1, 2]
    tasks = {}

    def task(name, fn, cond=None):
        tasks[name] = (fn, cond)

    def g(s, start, size):
        return gath.at[s, pl.ds(start, size)]

    def x_send(s, b):
        src = g(s, block_at(zn[order[b]], x, c), BLOCK)
        send(src, src, s_a.at[s], r_x.at[s, 0, b], up_x)
        send(src, src, s_a.at[s], r_x.at[s, 1, b], down_x)
        if s in ROUTED:
            send(src, src, s_a.at[s], r_x.at[s, 2, b], far_x)

    def a_own(s, n=None):
        if n is not None:
            if s == 3:

                @pl.when(lag == 2)
                def _():
                    gath[s, pl.ds(own, BLOCK), :] = ob[0]

            @pl.when(lag == 1)
            def _():
                gath[s, pl.ds(own, BLOCK), :] = ob[n]

        elif s == 0:
            load_h.wait()
        else:
            wait(g(s, own, BLOCK), r_shift.at[s])

    def a_start(s):
        src = g(s, own, BLOCK)
        send(src, src, s_a.at[s], r_z.at[s, 0], up_z)
        send(src, src, s_a.at[s], r_z.at[s, 1], down_z)
        send(src, src, s_a.at[s], r_z.at[s, 2], far_z)

    def shift():
        for s in (1, 2):
            @pl.when(lag + s < LAGS)
            def _():
                send(g(0, own, BLOCK), g(s, own, BLOCK), s_shift.at[s], r_shift.at[s], (lag_of(s), row))

    HALF = BLOCK // 2

    def to_mate(s, j, x_):
        src = g(s, chunk_of(x_, c), CHUNK)
        send(src, src, s_a.at[s], r_c.at[s, j], mate)

    def to_y(j, b):
        start = block_at(zn[order[b]], xn[order[j]], c)
        send(g(1, start, BLOCK), g(3, start, BLOCK), s_y.at[0], r_y.at[(0, 1, 1, 2)[j]], (lag_of(2), row))

    def from_y(i):
        wait(g(3, 0, (1, 2, 1)[i] * CHUNK), r_y.at[i])
        for j in ((0,), (1, 2), (3,))[i]:
            to_mate(3, j, xn[order[j]])

    def a_z(s, b):
        wait(g(s, block_at(zn[order[b]], x, c), BLOCK), r_z.at[s, b - 1])
        if b == 3:
            to_mate(s, 0, x)

    def a_x(s, b):
        zz = zn[order[b]]
        wait(g(s, block_at(zz, xn[3], c), BLOCK), r_x.at[s, 0, b])
        src = g(s, block_at(zz, xn[3], c), HALF)
        if s not in ROUTED:
            send(src, src, s_a.at[s], r_x.at[s, 2, b], up_x)
        wait(g(s, block_at(zz, xn[1], c), BLOCK), r_x.at[s, 1, b])
        src = g(s, block_at(zz, xn[1], c) + HALF, HALF)
        if s not in ROUTED:
            send(src, src, s_a.at[s], r_x.at[s, 2, b], down_x)
        if b == 3:
            to_mate(s, 1, xn[3])
            to_mate(s, 2, xn[1])

    def a_x_far(s):
        for b in range(4):
            wait(g(s, block_at(zn[order[b]], xn[2], c), BLOCK), r_x.at[s, 2, b])
        to_mate(s, 3, xn[2])

    def multiply(s, j):
        wait(g(s, chunk_of(xn[order[j]], 1 - c), CHUNK), r_c.at[s, j])

        def body(t, _):
            at_ = chunk_of(xn[order[j]], t)
            part[s] += jnp.dot(
                zv[:, pl.ds(at_, CHUNK)], gath[s, pl.ds(at_, CHUNK), :], preferred_element_type=jnp.float32
            )
            return 0

        lax.fori_loop(0, 2, body, 0)

    def w_cut():
        place = lax.broadcasted_iota(jnp.int32, (BLOCK, 128), 1) // PIECE

        def body(q, _):
            for half in range(2):
                tiles = []
                for b in range(4):
                    at_ = pl.multiple_of(q * CHUNK + b * BLOCK + half * 128, 128)
                    tile = zv[:, pl.ds(at_, 128)].astype(jnp.float32)
                    tiles.append(pltpu.roll(tile, PIECE * b, 1) if b else tile)
                for a in range(4):
                    got = tiles[(0 - a) % 4]
                    for p in range(1, 4):
                        got = jnp.where(place == p, tiles[(p - a) % 4], got)
                    zp[4 * half + a, :, pl.ds(pl.multiple_of(q * 128, 128), 128)] = got.astype(jnp.bfloat16)
            return 0

        lax.fori_loop(0, LAGS, body, 0)

    def w_send():
        pltpu.make_async_copy(zp.at[0], wv, r_w.at[0]).start()
        for k in (3, 7):
            send(zp.at[k], zp.at[0], s_w.at[0], r_w.at[1], (k - 1, row))
        for k in (4, 5, 2, 6, 1):
            send(zp.at[k], wv, s_w.at[0], r_w.at[0], (k, row))

    def w_relay():
        wait(zp.at[0], r_w.at[1])
        send(zp.at[0], wv, s_w.at[0], r_w.at[0], (lag_of(1), row))

    def rs_send(n):
        for k in FAR_FIRST:
            to = lag_of(k)
            send(
                part.at[n, pl.ds(pl.multiple_of(to * PIECE, PIECE), PIECE)],
                rsb.at[n, lag], s_rs.at[n], r_rs.at[n], (to, row),
            )
        rsb[n, lag] = part[n, pl.ds(piece, PIECE), :]

    def d_at(zh_, x_):
        return pl.multiple_of((c * 4 + x_) * 128 + ((zh_ + lag) % 4) * PIECE, PIECE)

    def new_density(n):
        wait(rsb.at[n, pl.ds(0, LAGS - 1)], r_rs.at[n])
        total = rsb[n, 0]
        for k in range(1, LAGS):
            total = total + rsb[n, k]
        drive = ev[n] - total
        density = (admit * drive / jnp.sqrt(1.0 + (satur * drive) ** 2)).astype(jnp.bfloat16)
        ob[n, pl.ds(piece, PIECE), :] = density
        if n < STEPS - 1:
            dv[n, pl.ds(d_at(zh, x), PIECE), :] = density
            src = dv.at[n, pl.ds(d_at(zh, x), PIECE)]
            send(src, src, s_d.at[n], r_dz.at[n, 0], far_z)
            send(src, src, s_d.at[n], r_dz.at[n, 1], up_z)
            send(src, src, s_d.at[n], r_dz.at[n, 2], down_z)
            d_send_x(n, 0)

    def out_send(n):
        src = ob.at[n, pl.ds(piece, PIECE)]
        for k in FAR_FIRST:
            send(src, src, s_o.at[n], r_o.at[n], (lag_of(k), row))

    def d_send_x(n, b):
        src = d_piece(n, b)
        for dev in (far_x, up_x, down_x):
            send(src, src, s_d.at[n], r_dx.at[n, b], dev)

    def d_piece(n, b):
        return dv.at[n, pl.ds(d_at(zn[order[b]], x), PIECE)]

    def d_near(n):
        wait(d_piece(n, 1), r_dz.at[n, 1])
        d_send_x(n, 1)
        wait(d_piece(n, 2), r_dz.at[n, 2])
        d_send_x(n, 2)

    def d_far(n):
        wait(d_piece(n, 3), r_dz.at[n, 0])
        d_send_x(n, 3)

    def d_c(n):
        for b in range(4):
            wait(dv.at[n, pl.ds(0, 3 * PIECE)], r_dx.at[n, b])
        src = dv.at[n, pl.ds(pl.multiple_of(c * 512, 512), 512)]
        send(src, src, s_d.at[n], r_dc.at[n], mate)

    def d_mul(n):
        wait(dv.at[n, pl.ds(0, 512)], r_dc.at[n])
        if n == 0:
            wait(wv, r_w.at[0])
        part[n + 1] += jnp.dot(wv[...], dv[n], preferred_element_type=jnp.float32)

    def o_ready(n):
        wait(ob.at[n, pl.ds(0, (LAGS - 1) * PIECE)], r_o.at[n])
        store(n).start()

    def store(n):
        return pltpu.make_async_copy(ob.at[n], out_hbm.at[n], s_out.at[n])

    def z_ready():
        wait(zv, s_loc.at[1])
        load_e.wait()

    task("shift", shift)
    task("z", z_ready)
    task("cut", w_cut, lag == 0)
    task("cut_out", w_send, lag == 0)
    task("relay", w_relay, (lag == 2) | (lag == 6))
    low = (lag == 1) | (lag == 2)
    gathers = ((0, None, None), (1, None, lag >= 1), (2, None, lag >= 2), (2, 0, lag == 1), (3, 1, low))
    for i, (s, n, cond) in enumerate(gathers):
        task(("own", i), functools.partial(a_own, s, n), cond)
        task(("start", i), functools.partial(a_start, s), cond)
        for b in range(4):
            task(("along_z", i, b), functools.partial(a_z, s, b), cond)
            task(("x", i, b), functools.partial(x_send, s, b), cond)
            task(("along_x", i, b), functools.partial(a_x, s, b), cond)
        task(("far_x", i), functools.partial(a_x_far, s), cond)
        for j in range(4):
            task(("mul", i, j), functools.partial(multiply, s, j), cond)
    for j in range(4):
        task(("mul", "y", j), functools.partial(multiply, 3, j), lag >= 3)
        for b in range(4):
            task(("y", j, b), functools.partial(to_y, j, b), (lag >= 1) & (lag + 2 < LAGS))
    for i in range(3):
        task(("along_y", i), functools.partial(from_y, i), lag >= 3)
    for n in range(STEPS):
        for name, fn in (
            ("sum", rs_send), ("density", new_density), ("out", out_send), ("outs", o_ready),
            ("near", d_near), ("far", d_far), ("mate", d_c), ("new", d_mul),
        ):
            task((name, n), functools.partial(fn, n))
    for name in ORDER:
        fn, cond = tasks[name]
        if cond is None:
            fn()
        else:
            pl.when(cond)(fn)

    for n in range(STEPS):
        wait(rsb.at[n, pl.ds(0, LAGS - 1)], s_rs.at[n])
        wait(ob.at[n, pl.ds(0, (LAGS - 1) * PIECE)], s_o.at[n])
        if n < STEPS - 1:
            wait(dv.at[n, pl.ds(0, 3 * PIECE + 12 * PIECE + 512)], s_d.at[n])
    for s in range(STEPS):
        def done(s=s):
            wait(g(s, 0, 3 * BLOCK + 12 * BLOCK + 4 * CHUNK), s_a.at[s])

        if s == 0:
            done()
        else:
            pl.when((lag >= 1) & (lag < 3) if s == 3 else lag >= 1)(done)
            if s == 3:
                @pl.when(lag >= 3)
                def _():
                    wait(g(s, 0, 4 * CHUNK), s_a.at[s])
                continue

            @pl.when(lag + s < LAGS)
            def _():
                wait(g(0, 0, BLOCK), s_shift.at[s])

    @pl.when((lag >= 1) & (lag + 2 < LAGS))
    def _():
        wait(g(3, 0, 4 * CHUNK), s_y.at[0])

    @pl.when((lag == 2) | (lag == 6))
    def _():
        wait(zp.at[0], s_w.at[0])

    @pl.when(lag == 0)
    def _():
        wait(zp.at[pl.ds(0, LAGS - 1)], s_w.at[0])

    for n in range(STEPS):
        store(n).wait()


def body(lag_matrices, history, excitation, admittance, saturation):
    dma = pltpu.SemaphoreType.DMA
    any_ = pl.BlockSpec(memory_space=pl.ANY)
    vmem = pl.BlockSpec(memory_space=pltpu.VMEM)
    return pl.pallas_call(
        kernel,
        out_shape=jax.ShapeDtypeStruct((STEPS, BLOCK, COLS), jnp.bfloat16),
        in_specs=[any_, any_, any_, vmem, vmem],
        out_specs=any_,
        scratch_shapes=[
            pltpu.VMEM((BLOCK, 8192), jnp.bfloat16),
            pltpu.VMEM((LAGS, BLOCK, CHUNK), jnp.bfloat16),
            pltpu.VMEM((BLOCK, CHUNK), jnp.bfloat16),
            pltpu.VMEM((STEPS, 8192, COLS), jnp.bfloat16),
            pltpu.VMEM((STEPS, BLOCK, COLS), jnp.float32),
            pltpu.VMEM((STEPS, LAGS, PIECE, COLS), jnp.float32),
            pltpu.VMEM((STEPS - 1, CHUNK, COLS), jnp.bfloat16),
            pltpu.VMEM((STEPS, BLOCK, COLS), jnp.bfloat16),
            pltpu.VMEM((STEPS, PIECE, COLS), jnp.float32),
            dma((3,)),
            dma((STEPS,)), dma((STEPS,)),
            dma((STEPS,)), dma((STEPS, 3)), dma((STEPS, 3, 4)), dma((STEPS, 4)),
            dma((1,)), dma((3,)),
            dma((1,)), dma((2,)),
            dma((STEPS,)), dma((STEPS,)),
            dma((STEPS,)), dma((STEPS, 3)), dma((STEPS, 4)), dma((STEPS,)),
            dma((STEPS,)), dma((STEPS,)),
            dma((STEPS,)),
        ],
        compiler_params=pltpu.CompilerParams(
            collective_id=0, has_side_effects=True, vmem_limit_bytes=60 * 1024 * 1024
        ),
    )(
        lag_matrices, history, excitation, admittance.reshape(1, BLOCK), saturation.reshape(1, BLOCK)
    )


def solution(mesh):
    placed = (
        P("lag", "row", None),
        P("lag", "row", None),
        P(None, "row", None),
        P("row"),
        P("row"),
    )
    return jax.shard_map(
        body, mesh=mesh, in_specs=placed, out_specs=P(None, "row", None), check_vma=False
    )
```

```python
import functools

import jax
import jax.numpy as jnp
from jax import lax
from jax.experimental import pallas as pl
from jax.experimental.pallas import tpu as pltpu
from jax.sharding import PartitionSpec as P

MESH = pl.DeviceIdType.MESH
STEPS = 4
LAGS = 8
BLOCK = 256
COLS = 256
ROUTED = (0,)
FAR_FIRST = (4, 5, 3, 2, 6, 1, 7)
ORDER = (
    ("own", 0), ("start", 0), ("x", 0, 0), "shift", "z", "cut", "cut_out", ("along_z", 0, 1), ("x", 0, 1),
    ("along_z", 0, 2), ("x", 0, 2), ("own", 1), ("start", 1), ("along_z", 0, 3), ("x", 0, 3), ("mul", 0, 0),
    ("x", 1, 0), ("along_z", 1, 1), ("along_z", 1, 2), ("x", 1, 1), ("y", 0, 0), "relay", ("along_z", 1, 3),
    ("y", 0, 1), ("x", 1, 2), ("along_x", 0, 0), ("along_x", 0, 1), ("along_x", 0, 2), ("along_x", 0, 3), ("mul", 0, 1),
    ("mul", 0, 2), ("far_x", 0), ("mul", 0, 3), ("sum", 0), ("y", 0, 2), ("mul", 1, 0), ("x", 1, 3), ("along_x", 1, 0),
    ("y", 0, 3), ("along_x", 1, 1), ("density", 0), ("out", 0), ("y", 1, 0), ("near", 0), ("along_x", 1, 2),
    ("y", 2, 0), ("far", 0), ("outs", 0), ("own", 2), ("start", 2), ("own", 3), ("start", 3), ("y", 1, 1),
    ("along_x", 1, 3), ("mate", 0), ("along_y", 0), ("mul", 1, 1), ("new", 0), ("mul", 1, 2), ("far_x", 1), ("x", 2, 0),
    ("x", 3, 0), ("mul", "y", 0), ("y", 2, 1), ("mul", 1, 3), ("sum", 1), ("along_z", 2, 1), ("x", 2, 1),
    ("along_z", 3, 1), ("x", 3, 1), ("along_z", 2, 2), ("along_z", 3, 2), ("y", 1, 2), ("x", 2, 2), ("x", 3, 2),
    ("y", 2, 2), ("along_z", 2, 3), ("along_z", 3, 3), ("along_x", 2, 0), ("density", 1), ("along_x", 3, 0), ("out", 1),
    ("mul", 2, 0), ("mul", 3, 0), ("near", 1), ("y", 1, 3), ("x", 2, 3), ("x", 3, 3), ("along_x", 2, 1),
    ("along_x", 3, 1), ("far", 1), ("outs", 1), ("y", 2, 3), ("own", 4), ("start", 4), ("along_x", 2, 2), ("mate", 1),
    ("along_x", 3, 2), ("y", 3, 0), ("new", 1), ("x", 4, 0), ("along_x", 2, 3), ("along_x", 3, 3), ("y", 3, 1),
    ("along_z", 4, 1), ("along_z", 4, 2), ("mul", 2, 1), ("mul", 3, 1), ("mul", 2, 2), ("mul", 3, 2), ("along_y", 1),
    ("far_x", 2), ("far_x", 3), ("x", 4, 1), ("mul", 2, 3), ("mul", 3, 3), ("sum", 2), ("along_x", 4, 0),
    ("mul", "y", 1), ("mul", "y", 2), ("y", 3, 2), ("along_z", 4, 3), ("x", 4, 2), ("mul", 4, 0), ("y", 3, 3),
    ("along_x", 4, 1), ("density", 2), ("out", 2), ("x", 4, 3), ("along_x", 4, 2), ("near", 2), ("along_y", 2),
    ("far", 2), ("outs", 2), ("along_x", 4, 3), ("mul", "y", 3), ("mul", 4, 1), ("mate", 2), ("mul", 4, 2),
    ("far_x", 4), ("new", 2), ("mul", 4, 3), ("sum", 3), ("density", 3), ("out", 3), ("outs", 3),
)
PIECE = 32
CHUNK = 1024


def kernel(
    z_hbm, h_hbm, e_hbm, adm_ref, sat_ref, out_hbm,
    zv, zp, wv, gath, part, rsb, dv, ob, ev,
    s_loc, s_shift, r_shift, s_a, r_z, r_x, r_c, s_y, r_y, s_w, r_w, s_rs, r_rs, s_d, r_dz, r_dx, r_dc, s_o, r_o, s_out,
):
    lag = lax.axis_index("lag")
    row = lax.axis_index("row")
    zh, x, c = row // 8, (row // 2) % 4, row % 2

    def at(zh_, x_, c_):
        return (lag, zh_ * 8 + x_ * 2 + c_)

    zn = [(zh + k) % 4 for k in range(4)]
    xn = [(x + k) % 4 for k in range(4)]
    up_z, down_z, far_z = at(zn[1], x, c), at(zn[3], x, c), at(zn[2], x, c)
    up_x, down_x, far_x = at(zh, xn[1], c), at(zh, xn[3], c), at(zh, xn[2], c)
    mate = at(zh, x, 1 - c)

    def lag_of(k):
        return (lag + k) % LAGS

    def chunk_of(x_, c_):
        return pl.multiple_of((c_ * 4 + x_) * CHUNK, CHUNK)

    def block_at(zh_, x_, c_):
        return pl.multiple_of(chunk_of(x_, c_) + zh_ * BLOCK, BLOCK)

    def send(src, dst, ss, rs, dev):
        pltpu.make_async_remote_copy(
            src_ref=src, dst_ref=dst, send_sem=ss, recv_sem=rs, device_id=dev, device_id_type=MESH
        ).start()

    def wait(ref, sem):
        pltpu.make_async_copy(ref, ref, sem).wait()

    own = block_at(zh, x, c)
    load_h = pltpu.make_async_copy(h_hbm.at[0], gath.at[0, pl.ds(own, BLOCK)], s_loc.at[0])
    load_h.start()

    def load_z(i, _):
        place = pl.multiple_of(((i % 2) * 16 + ((i // 2) % 4) * 4 + i // 8) * BLOCK, BLOCK)
        pltpu.make_async_copy(
            z_hbm.at[0, :, pl.ds(pl.multiple_of(i * BLOCK, BLOCK), BLOCK)],
            zv.at[:, pl.ds(place, BLOCK)],
            s_loc.at[1],
        ).start()
        return 0

    lax.fori_loop(0, 32, load_z, 0)
    piece = pl.multiple_of(lag * PIECE, PIECE)
    load_e = pltpu.make_async_copy(e_hbm.at[:, pl.ds(piece, PIECE)], ev, s_loc.at[2])
    load_e.start()

    barrier = pltpu.get_barrier_semaphore()
    partners = [up_z, down_z, far_z, up_x, down_x, far_x, mate] + [(lag_of(k), row) for k in range(1, LAGS)]
    for dev in partners:
        pl.semaphore_signal(barrier, inc=1, device_id=dev, device_id_type=MESH)
    part[...] = jnp.zeros_like(part)
    lanes = lax.broadcasted_iota(jnp.int32, (PIECE, BLOCK), 1)
    rows_ = lax.broadcasted_iota(jnp.int32, (PIECE, BLOCK), 0) + lag * PIECE
    mine = lanes == rows_
    admit = jnp.sum(jnp.where(mine, adm_ref[...], 0.0), axis=1, keepdims=True)
    satur = jnp.sum(jnp.where(mine, sat_ref[...], 0.0), axis=1, keepdims=True)
    pl.semaphore_wait(barrier, len(partners))

    order = [0, 3, 1, 2]
    tasks = {}

    def task(name, fn, cond=None):
        tasks[name] = (fn, cond)

    def g(s, start, size):
        return gath.at[s, pl.ds(start, size)]

    def x_send(s, b):
        src = g(s, block_at(zn[order[b]], x, c), BLOCK)
        send(src, src, s_a.at[s], r_x.at[s, 0, b], up_x)
        send(src, src, s_a.at[s], r_x.at[s, 1, b], down_x)
        if s in ROUTED:
            send(src, src, s_a.at[s], r_x.at[s, 2, b], far_x)

    def a_own(s, n=None):
        if n is not None:
            if s == 3:

                @pl.when(lag == 2)
                def _():
                    gath[s, pl.ds(own, BLOCK), :] = ob[0]

            @pl.when(lag == 1)
            def _():
                gath[s, pl.ds(own, BLOCK), :] = ob[n]

        elif s == 0:
            load_h.wait()
        else:
            wait(g(s, own, BLOCK), r_shift.at[s])

    def a_start(s):
        src = g(s, own, BLOCK)
        send(src, src, s_a.at[s], r_z.at[s, 0], up_z)
        send(src, src, s_a.at[s], r_z.at[s, 1], down_z)
        send(src, src, s_a.at[s], r_z.at[s, 2], far_z)

    def shift():
        for s in (1, 2):
            @pl.when(lag + s < LAGS)
            def _():
                send(g(0, own, BLOCK), g(s, own, BLOCK), s_shift.at[s], r_shift.at[s], (lag_of(s), row))

    HALF = BLOCK // 2

    def to_mate(s, j, x_):
        src = g(s, chunk_of(x_, c), CHUNK)
        send(src, src, s_a.at[s], r_c.at[s, j], mate)

    def to_y(j, b):
        start = block_at(zn[order[b]], xn[order[j]], c)
        send(g(1, start, BLOCK), g(3, start, BLOCK), s_y.at[0], r_y.at[(0, 1, 1, 2)[j]], (lag_of(2), row))

    def from_y(i):
        wait(g(3, 0, (1, 2, 1)[i] * CHUNK), r_y.at[i])
        for j in ((0,), (1, 2), (3,))[i]:
            to_mate(3, j, xn[order[j]])

    def a_z(s, b):
        wait(g(s, block_at(zn[order[b]], x, c), BLOCK), r_z.at[s, b - 1])
        if b == 3:
            to_mate(s, 0, x)

    def a_x(s, b):
        zz = zn[order[b]]
        wait(g(s, block_at(zz, xn[3], c), BLOCK), r_x.at[s, 0, b])
        src = g(s, block_at(zz, xn[3], c), HALF)
        if s not in ROUTED:
            send(src, src, s_a.at[s], r_x.at[s, 2, b], up_x)
        wait(g(s, block_at(zz, xn[1], c), BLOCK), r_x.at[s, 1, b])
        src = g(s, block_at(zz, xn[1], c) + HALF, HALF)
        if s not in ROUTED:
            send(src, src, s_a.at[s], r_x.at[s, 2, b], down_x)
        if b == 3:
            to_mate(s, 1, xn[3])
            to_mate(s, 2, xn[1])

    def a_x_far(s):
        for b in range(4):
            wait(g(s, block_at(zn[order[b]], xn[2], c), BLOCK), r_x.at[s, 2, b])
        to_mate(s, 3, xn[2])

    def multiply(s, j):
        wait(g(s, chunk_of(xn[order[j]], 1 - c), CHUNK), r_c.at[s, j])

        def body(t, _):
            at_ = chunk_of(xn[order[j]], t)
            part[s] += jnp.dot(
                zv[:, pl.ds(at_, CHUNK)], gath[s, pl.ds(at_, CHUNK), :], preferred_element_type=jnp.float32
            )
            return 0

        lax.fori_loop(0, 2, body, 0)

    def w_cut():
        place = lax.broadcasted_iota(jnp.int32, (BLOCK, 128), 1) // PIECE

        def body(q, _):
            for half in range(2):
                tiles = []
                for b in range(4):
                    at_ = pl.multiple_of(q * CHUNK + b * BLOCK + half * 128, 128)
                    tile = zv[:, pl.ds(at_, 128)].astype(jnp.float32)
                    tiles.append(pltpu.roll(tile, PIECE * b, 1) if b else tile)
                for a in range(4):
                    got = tiles[(0 - a) % 4]
                    for p in range(1, 4):
                        got = jnp.where(place == p, tiles[(p - a) % 4], got)
                    zp[4 * half + a, :, pl.ds(pl.multiple_of(q * 128, 128), 128)] = got.astype(jnp.bfloat16)
            return 0

        lax.fori_loop(0, LAGS, body, 0)

    def w_send():
        pltpu.make_async_copy(zp.at[0], wv, r_w.at[0]).start()
        for k in (3, 7):
            send(zp.at[k], zp.at[0], s_w.at[0], r_w.at[1], (k - 1, row))
        for k in (4, 5, 2, 6, 1):
            send(zp.at[k], wv, s_w.at[0], r_w.at[0], (k, row))

    def w_relay():
        wait(zp.at[0], r_w.at[1])
        send(zp.at[0], wv, s_w.at[0], r_w.at[0], (lag_of(1), row))

    def rs_send(n):
        for k in FAR_FIRST:
            to = lag_of(k)
            send(
                part.at[n, pl.ds(pl.multiple_of(to * PIECE, PIECE), PIECE)],
                rsb.at[n, lag], s_rs.at[n], r_rs.at[n], (to, row),
            )
        rsb[n, lag] = part[n, pl.ds(piece, PIECE), :]

    def d_at(zh_, x_):
        return pl.multiple_of((c * 4 + x_) * 128 + ((zh_ + lag) % 4) * PIECE, PIECE)

    def new_density(n):
        wait(rsb.at[n, pl.ds(0, LAGS - 1)], r_rs.at[n])
        total = rsb[n, 0]
        for k in range(1, LAGS):
            total = total + rsb[n, k]
        drive = ev[n] - total
        density = (admit * drive / jnp.sqrt(1.0 + (satur * drive) ** 2)).astype(jnp.bfloat16)
        ob[n, pl.ds(piece, PIECE), :] = density
        if n < STEPS - 1:
            dv[n, pl.ds(d_at(zh, x), PIECE), :] = density
            src = dv.at[n, pl.ds(d_at(zh, x), PIECE)]
            send(src, src, s_d.at[n], r_dz.at[n, 0], far_z)
            send(src, src, s_d.at[n], r_dz.at[n, 1], up_z)
            send(src, src, s_d.at[n], r_dz.at[n, 2], down_z)
            d_send_x(n, 0)

    def out_send(n):
        src = ob.at[n, pl.ds(piece, PIECE)]
        for k in FAR_FIRST:
            send(src, src, s_o.at[n], r_o.at[n], (lag_of(k), row))

    def d_send_x(n, b):
        src = d_piece(n, b)
        for dev in (far_x, up_x, down_x):
            send(src, src, s_d.at[n], r_dx.at[n, b], dev)

    def d_piece(n, b):
        return dv.at[n, pl.ds(d_at(zn[order[b]], x), PIECE)]

    def d_near(n):
        wait(d_piece(n, 1), r_dz.at[n, 1])
        d_send_x(n, 1)
        wait(d_piece(n, 2), r_dz.at[n, 2])
        d_send_x(n, 2)

    def d_far(n):
        wait(d_piece(n, 3), r_dz.at[n, 0])
        d_send_x(n, 3)

    def d_c(n):
        for b in range(4):
            wait(dv.at[n, pl.ds(0, 3 * PIECE)], r_dx.at[n, b])
        src = dv.at[n, pl.ds(pl.multiple_of(c * 512, 512), 512)]
        send(src, src, s_d.at[n], r_dc.at[n], mate)

    def d_mul(n):
        wait(dv.at[n, pl.ds(0, 512)], r_dc.at[n])
        if n == 0:
            wait(wv, r_w.at[0])
        part[n + 1] += jnp.dot(wv[...], dv[n], preferred_element_type=jnp.float32)

    def o_ready(n):
        wait(ob.at[n, pl.ds(0, (LAGS - 1) * PIECE)], r_o.at[n])
        store(n).start()

    def store(n):
        return pltpu.make_async_copy(ob.at[n], out_hbm.at[n], s_out.at[n])

    def z_ready():
        wait(zv, s_loc.at[1])
        load_e.wait()

    task("shift", shift)
    task("z", z_ready)
    task("cut", w_cut, lag == 0)
    task("cut_out", w_send, lag == 0)
    task("relay", w_relay, (lag == 2) | (lag == 6))
    low = (lag == 1) | (lag == 2)
    gathers = ((0, None, None), (1, None, lag >= 1), (2, None, lag >= 2), (2, 0, lag == 1), (3, 1, low))
    for i, (s, n, cond) in enumerate(gathers):
        task(("own", i), functools.partial(a_own, s, n), cond)
        task(("start", i), functools.partial(a_start, s), cond)
        for b in range(4):
            task(("along_z", i, b), functools.partial(a_z, s, b), cond)
            task(("x", i, b), functools.partial(x_send, s, b), cond)
            task(("along_x", i, b), functools.partial(a_x, s, b), cond)
        task(("far_x", i), functools.partial(a_x_far, s), cond)
        for j in range(4):
            task(("mul", i, j), functools.partial(multiply, s, j), cond)
    for j in range(4):
        task(("mul", "y", j), functools.partial(multiply, 3, j), lag >= 3)
        for b in range(4):
            task(("y", j, b), functools.partial(to_y, j, b), (lag >= 1) & (lag + 2 < LAGS))
    for i in range(3):
        task(("along_y", i), functools.partial(from_y, i), lag >= 3)
    for n in range(STEPS):
        for name, fn in (
            ("sum", rs_send), ("density", new_density), ("out", out_send), ("outs", o_ready),
            ("near", d_near), ("far", d_far), ("mate", d_c), ("new", d_mul),
        ):
            task((name, n), functools.partial(fn, n))
    for name in ORDER:
        fn, cond = tasks[name]
        if cond is None:
            fn()
        else:
            pl.when(cond)(fn)

    for n in range(STEPS):
        wait(rsb.at[n, pl.ds(0, LAGS - 1)], s_rs.at[n])
        wait(ob.at[n, pl.ds(0, (LAGS - 1) * PIECE)], s_o.at[n])
        if n < STEPS - 1:
            wait(dv.at[n, pl.ds(0, 3 * PIECE + 12 * PIECE + 512)], s_d.at[n])
    for s in range(STEPS):
        def done(s=s):
            wait(g(s, 0, 3 * BLOCK + 12 * BLOCK + 4 * CHUNK), s_a.at[s])

        if s == 0:
            done()
        else:
            pl.when((lag >= 1) & (lag < 3) if s == 3 else lag >= 1)(done)
            if s == 3:
                @pl.when(lag >= 3)
                def _():
                    wait(g(s, 0, 4 * CHUNK), s_a.at[s])
                continue

            @pl.when(lag + s < LAGS)
            def _():
                wait(g(0, 0, BLOCK), s_shift.at[s])

    @pl.when((lag >= 1) & (lag + 2 < LAGS))
    def _():
        wait(g(3, 0, 4 * CHUNK), s_y.at[0])

    @pl.when((lag == 2) | (lag == 6))
    def _():
        wait(zp.at[0], s_w.at[0])

    @pl.when(lag == 0)
    def _():
        wait(zp.at[pl.ds(0, LAGS - 1)], s_w.at[0])

    for n in range(STEPS):
        store(n).wait()


def body(lag_matrices, history, excitation, admittance, saturation):
    dma = pltpu.SemaphoreType.DMA
    any_ = pl.BlockSpec(memory_space=pl.ANY)
    vmem = pl.BlockSpec(memory_space=pltpu.VMEM)
    return pl.pallas_call(
        kernel,
        out_shape=jax.ShapeDtypeStruct((STEPS, BLOCK, COLS), jnp.bfloat16),
        in_specs=[any_, any_, any_, vmem, vmem],
        out_specs=any_,
        scratch_shapes=[
            pltpu.VMEM((BLOCK, 8192), jnp.bfloat16),
            pltpu.VMEM((LAGS, BLOCK, CHUNK), jnp.bfloat16),
            pltpu.VMEM((BLOCK, CHUNK), jnp.bfloat16),
            pltpu.VMEM((STEPS, 8192, COLS), jnp.bfloat16),
            pltpu.VMEM((STEPS, BLOCK, COLS), jnp.float32),
            pltpu.VMEM((STEPS, LAGS, PIECE, COLS), jnp.float32),
            pltpu.VMEM((STEPS - 1, CHUNK, COLS), jnp.bfloat16),
            pltpu.VMEM((STEPS, BLOCK, COLS), jnp.bfloat16),
            pltpu.VMEM((STEPS, PIECE, COLS), jnp.float32),
            dma((3,)),
            dma((STEPS,)), dma((STEPS,)),
            dma((STEPS,)), dma((STEPS, 3)), dma((STEPS, 3, 4)), dma((STEPS, 4)),
            dma((1,)), dma((3,)),
            dma((1,)), dma((2,)),
            dma((STEPS,)), dma((STEPS,)),
            dma((STEPS,)), dma((STEPS, 3)), dma((STEPS, 4)), dma((STEPS,)),
            dma((STEPS,)), dma((STEPS,)),
            dma((STEPS,)),
        ],
        compiler_params=pltpu.CompilerParams(
            collective_id=0, has_side_effects=True, vmem_limit_bytes=60 * 1024 * 1024
        ),
    )(
        lag_matrices, history, excitation, admittance.reshape(1, BLOCK), saturation.reshape(1, BLOCK)
    )


def solution(mesh):
    placed = (
        P("lag", "row", None),
        P("lag", "row", None),
        P(None, "row", None),
        P("row"),
        P("row"),
    )
    return jax.shard_map(
        body, mesh=mesh, in_specs=placed, out_specs=P(None, "row", None), check_vma=False
    )
```
